32 devices in a mesh: grp: 2 (over y), ep: 4 (over x, core), hid: 4 (over z).
Axes of the slice: x: 2, y: 2, z: 4, core: 2. Of those that a mesh axis runs over, the one named last changes fastest.
Arguments:
- tokens: bfloat16 [1024, 4096], P(('grp', 'ep')), parts along dimension 0, may hold values from -6 to 6
- expert_ids: int32 [1024, 2], P(('grp', 'ep')), parts along dimension 0, may hold values from 0 to 3, all different within a row; in each aligned block of 128 rows (0 to 127, 128 to 255, ...) at most 64 rows name the same one
- gate_probs: float32 [1024, 2], P(('grp', 'ep')), parts along dimension 0, may hold values from 0.05 to 1
- w_gate: bfloat16 [16, 4096, 384], P(('ep', 'hid')), may hold values from -0.09375 to 0.09375
- w_up: bfloat16 [16, 4096, 384], P(('ep', 'hid')), may hold values from -0.09375 to 0.09375
- w_down: bfloat16 [16, 384, 4096], P(('ep', 'hid')), may hold values from -0.15625 to 0.15625
Outputs:
- mixed_out: bfloat16 [1024, 4096], P(('grp', 'ep'), 'hid'), parts along dimension 0
The draws below stay inside these ranges and needn't reach their ends.
There are 2 independent parts, one for each index of `grp`. The reference program is written for one: setup_inputs(seed, part) draws one part's arguments, and reference() takes and returns one part's arrays. A program takes and returns all parts, laid end to end along the dimension named above; an argument that names none is the same for every part. Nothing has to cross between parts.
Inputs may be any that keep to these rules, and one draw needn't show every extreme that they name: `expert_ids`: each token names 2 different experts. Among the 128 tokens of one index of ep (aligned blocks of rows) no expert is named by more than 64 tokens, and in every draw some expert is named by exactly 64 tokens of some block.
All inputs are finite; a program needn't handle non-finite values.
Results may differ from the reference program's by a relative error of at most 0.0085.
Values may be sent and summed in bfloat16 or wider, within the bound.
No kernel may reach another device: no remote copies, remote signals or barrier semaphores. Data moves between devices by JAX's collectives and lax.ppermute only.
A program may use at most 128 MiB of HBM per device.

```python
import math
import jax
import jax.numpy as jnp
import numpy as np
from jax import lax

D = 4096
HIDDEN_SIZE = 1536
QUARTERS = 4
TOK_EP = 128
EXPERTS = 4
TOP = 2
CAP = 64
TOKENS = 512
N_EP = 4


def levels(own_key, dims, split, smallest, largest):
    def one(dim, blocks):
        steps = jax.random.uniform(jax.random.fold_in(jax.random.fold_in(own_key, 6), dim), (blocks,), jnp.float32, smallest / len(split), largest / len(split))
        return jnp.repeat(jnp.exp(steps), dims[dim] // blocks).reshape((-1,) + (1,) * (len(dims) - dim - 1))

    loudness = one(*split[0])
    for cut in split[1:]:
        loudness = loudness * one(*cut)
    return loudness


def shared_out(own_key, own, number, rows, count, top, most, lean):
    order = jax.random.permutation(own_key, count)
    crowded, common = shares(count, rows * top, most, lean, True), shares(count, rows * top, most, lean, False)
    places = jnp.arange(count)

    def named(tallies, turn):
        used = int((tallies > 0).sum())
        fixed = max(1, used // 4)
        passed = fixed + (places - fixed + turn * (used - fixed)) % max(1, count - fixed)
        return jnp.zeros((count,), jnp.int32).at[order[jnp.where(places < fixed, places, passed)]].set(jnp.asarray(tallies, jnp.int32))

    tallies = jnp.where(number % 4 == 0, named(crowded, number // 4), named(common, number - number // 4 - 1))
    mixed = jax.random.permutation(jax.random.fold_in(own, 3), count)
    donor, sink = mixed[0:count // 2 * 2:2], mixed[1:count // 2 * 2:2]
    room = jnp.minimum(tallies[donor] - 1, most - tallies[sink]) // 2
    room = jnp.where((donor == order[0]) | (sink == order[0]) | (tallies[sink] == 0), 0, jnp.maximum(room, 0))
    passed = jax.random.randint(jax.random.fold_in(own, 4), (count // 2,), 0, 1 << 20) % (room + 1)
    tallies = tallies.at[donor].add(-passed).at[sink].add(passed)
    items = jnp.searchsorted(jnp.cumsum(tallies), jnp.arange(rows * top), side="right").astype(jnp.int32)
    listing = items.reshape(top, rows).T
    listing = listing[jax.random.permutation(jax.random.fold_in(own, 1), rows)]
    turn = jax.random.randint(jax.random.fold_in(own, 2), (rows, 1), 0, top)
    return jnp.take_along_axis(listing, (jnp.arange(top)[None, :] + turn) % top, axis=1)


def shares(count, total, reach, slope, full):
    loads = [(1 << 20) // math.isqrt(standing ** slope) + 1 for standing in range(1, count + 1)]
    largest = reach if full else min(reach, max(-(-total // count), total * loads[0] // sum(loads)))
    least = 1 if total - largest >= count - 1 else 0
    given, rest = [largest] + [least] * (count - 1), total - largest - least * (count - 1)
    while rest > 0:
        movable = [i for i in range(1, count) if given[i] < largest] or [i for i in range(1, count) if given[i] < reach]
        pool, left = sum([loads[i] for i in movable]), rest
        for i in movable:
            extra = min(reach - given[i], max(1, left * loads[i] // pool), rest)
            given[i] = given[i] + extra
            rest = rest - extra
    return np.array(given)


def noise(own_key, extent, width, most, cuts=(), kind=jnp.bfloat16):
    array = width * jax.random.normal(own_key, extent, jnp.float32)
    if cuts:
        array = array * levels(own_key, extent, cuts, -0.22, 0.18)
    return jnp.clip(array, -most, most).astype(kind)


def setup_inputs(seed: int = 0, part: int = 0) -> dict:
    keys = jax.random.split(jax.random.key(seed), 7)
    part_keys = jax.random.split(jax.random.fold_in(keys[6], part), 7)
    tokens = noise(part_keys[0], (TOKENS, D), 1.0, 6.0, ((0, 4),))
    expert_ids_keys = jax.random.split(jax.random.fold_in(part_keys[1], 1), TOKENS // TOK_EP)
    expert_ids_turns = jax.random.permutation(jax.random.fold_in(part_keys[1], 3), TOKENS // TOK_EP)
    expert_ids = jax.vmap(lambda own, number: shared_out(jax.random.fold_in(part_keys[1], 2), own, number, TOK_EP, EXPERTS, TOP, CAP, 2))(expert_ids_keys, expert_ids_turns).reshape((TOKENS, TOP))
    gate_probs = jnp.clip(jnp.exp(math.log(1.0) - 2.9957323 * jax.random.uniform(part_keys[2], (TOKENS, TOP), jnp.float32) ** levels(part_keys[2], (TOKENS, TOP), ((0, 4),), -0.2, 0.2)), 0.05, 1.0)
    w_gate = noise(keys[3], (EXPERTS * QUARTERS, D, HIDDEN_SIZE // QUARTERS), D ** -0.5, 0.09375, ((0, 16),))
    w_up = noise(keys[4], (EXPERTS * QUARTERS, D, HIDDEN_SIZE // QUARTERS), D ** -0.5, 0.09375, ((0, 16),))
    w_down = noise(keys[5], (EXPERTS * QUARTERS, HIDDEN_SIZE // QUARTERS, D), HIDDEN_SIZE ** -0.5, 0.15625, ((0, 16),))
    return {"tokens": tokens, "expert_ids": expert_ids, "gate_probs": gate_probs, "w_gate": w_gate, "w_up": w_up, "w_down": w_down}


def reference(tokens, expert_ids, gate_probs, w_gate, w_up, w_down):
    tok_total, model_width = tokens.shape
    pick_count = expert_ids.shape[1]
    experts = w_gate.shape[0] // QUARTERS
    quarter_width = w_gate.shape[2]
    slots_each = N_EP * CAP
    grouped = expert_ids.reshape(N_EP, TOK_EP * pick_count)
    onehot = (grouped[:, :, None] == jnp.arange(experts, dtype=jnp.int32)[None, None, :]).astype(jnp.int32)
    before = jnp.cumsum(onehot, axis=1) - onehot
    position = jnp.sum(before * onehot, axis=2).astype(jnp.int32)
    block_index = jnp.arange(N_EP, dtype=jnp.int32)[:, None]
    slot_index = (grouped * slots_each + block_index * CAP + position).reshape(-1).astype(jnp.int32)
    routed_rows = jnp.repeat(tokens, pick_count, axis=0)
    buffer = jnp.zeros((experts * slots_each, model_width), tokens.dtype)
    buffer = buffer.at[slot_index].set(routed_rows).reshape(experts, slots_each, model_width)
    gate_stack = w_gate.reshape(experts, QUARTERS, model_width, quarter_width)
    up_stack = w_up.reshape(experts, QUARTERS, model_width, quarter_width)
    down_stack = w_down.reshape(experts, QUARTERS, quarter_width, model_width)

    def expert_fn(operands):
        expert_rows, gate_matrix, up_matrix, down_matrix = operands
        running = jnp.zeros((expert_rows.shape[0], model_width), jnp.float32)
        for index in range(QUARTERS):
            gate_act = jnp.dot(expert_rows, gate_matrix[index], preferred_element_type=jnp.float32)
            up_act = jnp.dot(expert_rows, up_matrix[index], preferred_element_type=jnp.float32)
            hidden = (jax.nn.silu(gate_act) * up_act).astype(jnp.bfloat16)
            piece_sum = jnp.dot(hidden, down_matrix[index], preferred_element_type=jnp.float32).astype(jnp.bfloat16)
            running = running + lax.optimization_barrier(piece_sum).astype(jnp.float32)
        return running

    outputs = lax.map(expert_fn, (buffer, gate_stack, up_stack, down_stack))
    picked = outputs.reshape(-1, model_width)[slot_index].reshape(tok_total, pick_count, model_width)
    weights = lax.optimization_barrier(gate_probs.astype(jnp.bfloat16)).astype(jnp.float32)
    mixed_out = jnp.einsum('tk,tkd->td', weights, picked, precision=lax.Precision.HIGHEST)
    return mixed_out.astype(jnp.bfloat16)
```

```python
import jax
import jax.numpy as jnp
from jax import lax
from jax.sharding import PartitionSpec as P

QUARTERS = 4


def swap(value, axis, offset):
    return lax.ppermute(value, axis, [(i, i ^ offset) for i in range(lax.axis_size(axis))])


def local(tokens, expert_ids, gate_probs, w_gate, w_up, w_down):
    ep_count = lax.axis_size("ep")
    hid_count = lax.axis_size("hid")
    tok_rows, model_width = tokens.shape
    groups = hid_count // QUARTERS
    capacity = tok_rows // 2
    hid_index = lax.axis_index("hid")
    offsets = jnp.arange(ep_count, dtype=jnp.int32)
    experts = (lax.axis_index("ep") ^ offsets) * groups + hid_index // QUARTERS
    hit = expert_ids[:, :, None] == experts[None, None, :]
    hot = jnp.any(hit, axis=1)
    earlier = jnp.tril(jnp.ones((tok_rows, tok_rows), jnp.bfloat16), -1)
    position = jnp.dot(earlier, hot.astype(jnp.bfloat16), preferred_element_type=jnp.float32)
    position = position.astype(jnp.int32)
    gate_round = gate_probs.astype(jnp.bfloat16).astype(jnp.float32)
    gates = jnp.sum(jnp.where(hit, gate_round[:, :, None], 0.0), axis=1)
    slots = jnp.arange(capacity, dtype=jnp.int32)
    match = hot[:, :, None] & (position[:, :, None] == slots)
    scatter = match.astype(jnp.bfloat16)
    combine = jnp.where(match, gates[:, :, None], 0.0).astype(jnp.bfloat16)

    def dispatch(offset):
        rows = lax.dot_general(
            scatter[:, offset],
            tokens,
            (((0,), (0,)), ((), ())),
            preferred_element_type=jnp.float32,
        )
        return rows.astype(jnp.bfloat16)

    def expert(rows):
        gate_act = jnp.dot(rows, w_gate[0], preferred_element_type=jnp.float32)
        up_act = jnp.dot(rows, w_up[0], preferred_element_type=jnp.float32)
        hidden = (jax.nn.silu(gate_act) * up_act).astype(jnp.bfloat16)
        return jnp.dot(hidden, w_down[0], preferred_element_type=jnp.float32).astype(jnp.bfloat16)

    def reduce(partial):
        rows = partial.shape[0]
        blocks = partial.reshape(rows, hid_count, -1)
        bit = 1
        while bit < hid_count:
            pairs = blocks.reshape(rows, -1, 2, blocks.shape[-1])
            upper = (hid_index // bit) % 2 == 1
            keep = jnp.where(upper, pairs[:, :, 1], pairs[:, :, 0])
            send = jnp.where(upper, pairs[:, :, 0], pairs[:, :, 1])
            got = swap(send, "hid", bit)
            blocks = (keep.astype(jnp.float32) + got.astype(jnp.float32)).astype(jnp.bfloat16)
            bit *= 2
        return blocks.reshape(rows, -1)

    arrived = {offset: swap(dispatch(offset), "ep", offset) for offset in range(2, ep_count)}
    arrived[1] = swap(dispatch(1), "ep", 1)
    arrived[0] = dispatch(0)
    returned = {}
    for offset in range(ep_count):
        summed = reduce(expert(arrived[offset]))
        returned[offset] = swap(summed, "ep", offset) if offset else summed
    stacked = jnp.concatenate([returned[offset] for offset in range(ep_count)], axis=0)
    mixed_out = jnp.dot(
        combine.reshape(tok_rows, -1), stacked, preferred_element_type=jnp.float32
    )
    return mixed_out.astype(jnp.bfloat16)


def solution(mesh):
    in_specs = (
        P(("grp", "ep"), None),
        P(("grp", "ep"), None),
        P(("grp", "ep"), None),
        P(("ep", "hid"), None, None),
        P(("ep", "hid"), None, None),
        P(("ep", "hid"), None, None),
    )
    out_specs = P(("grp", "ep"), "hid")
    return jax.shard_map(local, mesh=mesh, in_specs=in_specs, out_specs=out_specs, check_vma=False)
```
